512 devices in a mesh: rows: 128 (over y, z, core), cols: 4 (over x).
Axes of the slice: x: 4, y: 4, z: 16, core: 2. Of those that a mesh axis runs over, the one named last changes fastest.
Arguments:
- prior: bfloat16 [2048, 16, 128, 128], P('rows', 'cols'), may hold values from -6 to 6
- candidates: int32 [2048, 16], P('rows', 'cols'), may hold values from 0 to 2047, as said below
- cross_link: int32 [2048], P(('rows', 'cols')), may hold values from 0 to 2047, as said below
- a1_blocks: bfloat16 [2048, 2, 128, 128], P(('rows', 'cols')), may hold values from -0.375 to 0.375
- a2_blocks: bfloat16 [2048, 128, 128], P(('rows', 'cols')), may hold values from -0.5 to 0.5
Outputs:
- similarity: bfloat16 [2048, 16, 128, 128], P('rows', 'cols')
The draws below stay inside these ranges and needn't reach their ends.
Inputs may be any that keep to these rules, and one draw needn't show every extreme that they name: Target block t lies in target slab t // 16 and quarter (t // 4) % 4; a candidate in columns q * 4 to (q + 1) * 4 - 1 names a target of quarter q. The candidates of one row block in one quarter lie in distinct target slabs. Of the candidates held by one device, at most 1 lie in one target slab, and some slab gets exactly 1; every target slab gets 16 * 4 candidates of its quarter from all source slabs together. `cross_link`: the linked row block of a row block in slab r lies in the last half of the row blocks of slab (r + 1) % 128.
All inputs are finite; a program needn't handle non-finite values.
Results may differ from the reference program's by a relative error of at most 0.006.
Values may be sent and summed in bfloat16 or wider, within the bound.
A program may use at most 64 MiB of HBM per device.

```python
import jax
import jax.numpy as jnp
from jax import lax

B = 128
K = 16
RBD = 16
KQ = 4
TBD = 4
RB = 2048
N_ROWS = 128
N_COLS = 4


def draw_candidates(key, part):
    key_shift = jax.random.fold_in(key, 11)
    key_table = jax.random.fold_in(key, 12)
    key_order = jax.random.fold_in(key, 13)
    row_index = jnp.arange(RB, dtype=jnp.int32)
    column_step = jnp.arange(KQ, dtype=jnp.int32)
    quarter = jnp.arange(N_COLS, dtype=jnp.int32)[None, :, None]
    shifts = jax.random.randint(key_shift, (N_COLS,), 0, N_ROWS, dtype=jnp.int32)
    table = jax.random.randint(key_table, (N_COLS, N_ROWS * TBD), 0, TBD, dtype=jnp.int32)
    code = row_index[:, None, None] + (RBD + 1) * column_step[None, None, :]
    code = jnp.broadcast_to(code, (RB, N_COLS, KQ))
    dest_slab = (code + shifts[None, :, None]) % N_ROWS
    local_index = table[jnp.broadcast_to(quarter, (RB, N_COLS, KQ)), code % (N_ROWS * TBD)]
    target = dest_slab * (N_COLS * TBD) + quarter * TBD + local_index
    scores = jax.random.randint(key_order, (RB, N_COLS, KQ), 0, 1048576, dtype=jnp.int32) * KQ + column_step[None, None, :]
    order = jnp.argsort(scores, axis=2)
    target = jnp.take_along_axis(target, order, axis=2)
    return target.reshape(RB, K).astype(jnp.int32)


def draw_cross_link(key, part):
    key_coin = jax.random.fold_in(key, 21)
    key_pick = jax.random.fold_in(key, 22)
    row_index = jnp.arange(RB, dtype=jnp.int32)
    slab_index = row_index // RBD
    within_slab = row_index % RBD
    next_slab = (slab_index + 1) % N_ROWS
    coin = jax.random.randint(key_coin, (RB,), 0, 4, dtype=jnp.int32)
    random_pick = jax.random.randint(key_pick, (RB,), RBD // 2, RBD, dtype=jnp.int32)
    aligned = (within_slab >= RBD // 2 - 1) & (within_slab <= RBD - 2) & (coin > 0)
    chosen_row = jnp.where(aligned, within_slab + 1, random_pick)
    return (next_slab * RBD + chosen_row).astype(jnp.int32)


def levels(rng, shape, shards, least, largest):
    def one(position, shards_of):
        steps = jax.random.uniform(jax.random.fold_in(jax.random.fold_in(rng, 6), position), (shards_of,), jnp.float32, least / len(shards), largest / len(shards))
        return jnp.repeat(jnp.exp(steps), shape[position] // shards_of).reshape((-1,) + (1,) * (len(shape) - position - 1))

    gain = one(*shards[0])
    for cut in shards[1:]:
        gain = gain * one(*cut)
    return gain


def centred(rng, dims, deviation, limit, split=(), held_as=jnp.bfloat16):
    result = deviation * jax.random.normal(rng, dims, jnp.float32)
    if split:
        result = result * levels(rng, dims, split, -0.22, 0.18)
    return jnp.clip(result, -limit, limit).astype(held_as)


def setup_inputs(seed: int = 0) -> dict:
    seeds = jax.random.split(jax.random.key(seed), 6)
    prior = centred(seeds[0], (RB, K, B, B), 1.0, 6.0, ((0, 128), (1, 4)))
    candidates = draw_candidates(jax.random.fold_in(seeds[5], 71), 0)
    cross_link = draw_cross_link(jax.random.fold_in(seeds[5], 71), 0)
    a1_blocks = centred(seeds[3], (RB, 2, B, B), (2 * B) ** -0.5, 0.375, ((0, 512),))
    a2_blocks = centred(seeds[4], (RB, B, B), B ** -0.5, 0.5, ((0, 512),))
    return {"prior": prior, "candidates": candidates, "cross_link": cross_link, "a1_blocks": a1_blocks, "a2_blocks": a2_blocks}


mixing = 0.75


def left_slab(values, offset, prior_ids, cross_link, a1_blocks):
    slab_vals = lax.dynamic_slice_in_dim(values, offset, RBD, 0)
    slab_ids = lax.dynamic_slice_in_dim(prior_ids, offset, RBD, 0)
    adjacency = lax.dynamic_slice_in_dim(a1_blocks, offset, RBD, 0)
    neighbour = lax.dynamic_slice_in_dim(cross_link, offset, RBD, 0)
    nb_values = values[neighbour]
    nb_ids = prior_ids[neighbour]
    matches = slab_ids[:, :, None] == nb_ids[:, None, :]
    chosen = jnp.sum(jnp.where(matches, jnp.arange(K, dtype=jnp.int32)[None, None, :], 0), axis=2).astype(jnp.int32)
    found = jnp.any(matches, axis=2)
    picked = jnp.take_along_axis(nb_values, chosen[:, :, None, None], axis=1)
    picked = jnp.where(found[:, :, None, None], picked, jnp.zeros_like(picked))
    own_term = jnp.einsum("ixy,ikyz->ikxz", adjacency[:, 0].astype(jnp.float32), slab_vals.astype(jnp.float32), precision=lax.Precision.HIGHEST)
    cross_term = jnp.einsum("ixy,ikyz->ikxz", adjacency[:, 1].astype(jnp.float32), picked.astype(jnp.float32), precision=lax.Precision.HIGHEST)
    return own_term + cross_term


def right_blocks(slab_vals, slab_ids, a2_blocks):
    target_blocks = a2_blocks[slab_ids]
    return jnp.einsum("ikxy,ikzy->ikxz", slab_vals.astype(jnp.float32), target_blocks.astype(jnp.float32), precision=lax.Precision.HIGHEST)


def reference(prior, candidates, cross_link, a1_blocks, a2_blocks):
    offsets = jnp.arange(N_ROWS, dtype=jnp.int32) * RBD

    def phase_one(offset):
        return left_slab(prior, offset, candidates, cross_link, a1_blocks).astype(jnp.bfloat16)

    first = lax.map(phase_one, offsets).reshape(RB, K, B, B)

    def phase_two(offset):
        slab_first = lax.dynamic_slice_in_dim(first, offset, RBD, 0)
        slab_prior = lax.dynamic_slice_in_dim(prior, offset, RBD, 0)
        slab_ids = lax.dynamic_slice_in_dim(candidates, offset, RBD, 0)
        image = right_blocks(slab_first, slab_ids, a2_blocks)
        swept = (mixing * image + (1.0 - mixing) * slab_prior.astype(jnp.float32)).astype(jnp.bfloat16)
        return right_blocks(swept, slab_ids, a2_blocks).astype(jnp.bfloat16)

    carried = lax.map(phase_two, offsets).reshape(RB, K, B, B)

    def phase_three(offset):
        slab_prior = lax.dynamic_slice_in_dim(prior, offset, RBD, 0)
        image = left_slab(carried, offset, candidates, cross_link, a1_blocks)
        return (mixing * image + (1.0 - mixing) * slab_prior.astype(jnp.float32)).astype(jnp.bfloat16)

    return lax.map(phase_three, offsets).reshape(RB, K, B, B)
```

```python
import jax
import jax.numpy as jnp
from jax import lax
from jax.experimental import pallas as pl
from jax.experimental.pallas import tpu as pltpu
from jax.sharding import PartitionSpec as P

mixing = 0.75


def passed_along(array, axis, by):
    count = lax.axis_size(axis)
    return lax.ppermute(array, axis, [(i, (i + by) % count) for i in range(count)])


def contract(a, b, dims):
    return lax.dot_general(a, b, (dims, ((), ())), preferred_element_type=jnp.float32)


def left_kernel(within, chosen, found, prior, next_prior, adjacency, first):
    rows, per = prior.shape[0], prior.shape[1]

    def step(i, carry):
        for k in range(per):
            n = i * per + k
            picked = next_prior[within[i], chosen[n]]
            picked = jnp.where(found[n] > 0, picked, jnp.zeros_like(picked))
            total = contract(adjacency[i, 0], prior[i, k], ((1,), (0,)))
            total = total + contract(adjacency[i, 1], picked, ((1,), (0,)))
            first[i, k] = total.astype(jnp.bfloat16)
        return carry

    lax.fori_loop(0, rows, step, 0)


def sweep_kernel(
    within, chosen, found, place, prior, next_prior, first, next_first, adjacency, a2, out, blocks, sems
):
    rows, per = prior.shape[0], prior.shape[1]

    def fetch(n):
        return pltpu.make_async_copy(a2.at[place[n]], blocks.at[n], sems.at[n])

    def begin(n, carry):
        fetch(n).start()
        return carry

    lax.fori_loop(0, rows * per, begin, 0)

    def step(i, carry):
        for k in range(per):
            fetch(i * per + k).wait()
        for k in range(per):
            n = i * per + k
            keep = found[n] > 0
            picked_prior = next_prior[within[i], chosen[n]]
            picked_first = next_first[within[i], chosen[n]]
            zero = jnp.zeros_like(picked_prior)
            picked_prior = jnp.where(keep, picked_prior, zero)
            picked_first = jnp.where(keep, picked_first, zero)
            own_prior = prior[i, k]
            target = blocks[n]
            values = jnp.concatenate([first[i, k], picked_first], axis=0)
            base = jnp.concatenate([own_prior, picked_prior], axis=0).astype(jnp.float32)
            image = contract(values, target, ((1,), (1,)))
            swept = (mixing * image + (1.0 - mixing) * base).astype(jnp.bfloat16)
            carried = contract(swept, target, ((1,), (1,))).astype(jnp.bfloat16)
            block = own_prior.shape[0]
            total = contract(adjacency[i, 0], carried[:block], ((1,), (0,)))
            total = total + contract(adjacency[i, 1], carried[block:], ((1,), (0,)))
            out[i, k] = (mixing * total + (1.0 - mixing) * own_prior.astype(jnp.float32)).astype(
                jnp.bfloat16
            )
        return carry

    lax.fori_loop(0, rows, step, 0)


def local(prior, candidates, cross_link, a1_blocks, a2_blocks):
    row_blocks, per_quarter, block = prior.shape[0], prior.shape[1], prior.shape[2]
    targets_here = a2_blocks.shape[0]
    column_count = lax.axis_size("cols")
    upper_half = row_blocks // 2
    smem = pl.BlockSpec(memory_space=pltpu.SMEM)
    vmem = pl.BlockSpec(memory_space=pltpu.VMEM)
    adjacency = lax.all_gather(a1_blocks, "cols", axis=0, tiled=True)
    links = lax.all_gather(cross_link, "cols", axis=0, tiled=True)
    targets = lax.all_gather(a2_blocks, "rows", axis=0, tiled=True)
    within = links % row_blocks - upper_half
    next_ids = passed_along(candidates[upper_half:], "rows", -1)
    next_prior = passed_along(prior[upper_half:], "rows", -1)
    matches = candidates[:, :, None] == next_ids[within][:, None, :]
    chosen = jnp.sum(
        jnp.where(matches, jnp.arange(per_quarter, dtype=jnp.int32)[None, None, :], 0), axis=2
    ).reshape(-1)
    found = jnp.any(matches, axis=2).astype(jnp.int32).reshape(-1)
    place = (
        candidates // (column_count * targets_here) * targets_here + candidates % targets_here
    ).reshape(-1)
    shape = jax.ShapeDtypeStruct(prior.shape, jnp.bfloat16)
    flops = 2 * row_blocks * per_quarter * block**3
    first = pl.pallas_call(
        left_kernel,
        out_shape=shape,
        in_specs=[smem, smem, smem, vmem, vmem, vmem],
        out_specs=vmem,
        cost_estimate=pl.CostEstimate(
            flops=2 * flops, bytes_accessed=4 * prior.size * 2, transcendentals=0
        ),
    )(within, chosen, found, prior, next_prior, adjacency)
    next_first = passed_along(first[upper_half:], "rows", -1)
    return pl.pallas_call(
        sweep_kernel,
        out_shape=shape,
        in_specs=[smem] * 4 + [vmem] * 5 + [pl.BlockSpec(memory_space=pl.ANY)],
        out_specs=vmem,
        scratch_shapes=[
            pltpu.VMEM((row_blocks * per_quarter, block, block), jnp.bfloat16),
            pltpu.SemaphoreType.DMA((row_blocks * per_quarter,)),
        ],
        cost_estimate=pl.CostEstimate(
            flops=6 * flops, bytes_accessed=6 * prior.size * 2, transcendentals=0
        ),
    )(within, chosen, found, place, prior, next_prior, first, next_first, adjacency, targets)


def solution(mesh):
    placed = (
        P("rows", "cols", None, None),
        P("rows", "cols"),
        P(("rows", "cols")),
        P(("rows", "cols"), None, None, None),
        P(("rows", "cols"), None, None),
    )
    return jax.shard_map(
        local, mesh=mesh, in_specs=placed, out_specs=P("rows", "cols", None, None), check_vma=False
    )
```

```python
import jax
import jax.numpy as jnp
from jax import lax
from jax.experimental import pallas as pl
from jax.experimental.pallas import tpu as pltpu
from jax.sharding import PartitionSpec as P

mixing = 0.75


def passed_along(array, axis, by):
    count = lax.axis_size(axis)
    return lax.ppermute(array, axis, [(i, (i + by) % count) for i in range(count)])


def contract(a, b, dims):
    return lax.dot_general(a, b, (dims, ((), ())), preferred_element_type=jnp.float32)


def left_kernel(within, chosen, found, prior, next_prior, adjacency, first):
    rows, per = prior.shape[0], prior.shape[1]

    def step(i, carry):
        for k in range(per):
            n = i * per + k
            picked = next_prior[within[i], chosen[n]]
            picked = jnp.where(found[n] > 0, picked, jnp.zeros_like(picked))
            total = contract(adjacency[i, 0], prior[i, k], ((1,), (0,)))
            total = total + contract(adjacency[i, 1], picked, ((1,), (0,)))
            first[i, k] = total.astype(jnp.bfloat16)
        return carry

    lax.fori_loop(0, rows, step, 0)


def sweep_kernel(
    within, chosen, found, place, prior, next_prior, first, next_first, adjacency, a2, out, blocks, sems
):
    rows, per = prior.shape[0], prior.shape[1]

    def fetch(n):
        return pltpu.make_async_copy(a2.at[place[n]], blocks.at[n], sems.at[n])

    def begin(n, carry):
        fetch(n).start()
        return carry

    lax.fori_loop(0, rows * per, begin, 0)

    def step(i, carry):
        for k in range(per):
            fetch(i * per + k).wait()
        for k in range(per):
            n = i * per + k
            keep = found[n] > 0
            picked_prior = next_prior[within[i], chosen[n]]
            picked_first = next_first[within[i], chosen[n]]
            zero = jnp.zeros_like(picked_prior)
            picked_prior = jnp.where(keep, picked_prior, zero)
            picked_first = jnp.where(keep, picked_first, zero)
            own_prior = prior[i, k]
            target = blocks[n]
            values = jnp.concatenate([first[i, k], picked_first], axis=0)
            base = jnp.concatenate([own_prior, picked_prior], axis=0).astype(jnp.float32)
            image = contract(values, target, ((1,), (1,)))
            swept = (mixing * image + (1.0 - mixing) * base).astype(jnp.bfloat16)
            carried = contract(swept, target, ((1,), (1,))).astype(jnp.bfloat16)
            block = own_prior.shape[0]
            total = contract(adjacency[i, 0], carried[:block], ((1,), (0,)))
            total = total + contract(adjacency[i, 1], carried[block:], ((1,), (0,)))
            out[i, k] = (mixing * total + (1.0 - mixing) * own_prior.astype(jnp.float32)).astype(
                jnp.bfloat16
            )
        return carry

    lax.fori_loop(0, rows, step, 0)

MESH = pl.DeviceIdType.MESH
ny, nz, cores = 4, 16, 2


def gather_kernel(
    a2, whole, own_sem, az_s, az_r, bz_s, bz_r, by_s, by_r, ay_s, ay_r, ah_s, ah_r, sib_s, sib_r
):
    me, col = lax.axis_index("rows"), lax.axis_index("cols")
    core = lax.rem(me, cores)
    z = lax.rem(me // cores, nz)
    y = me // (cores * nz)
    height = a2.shape[0]
    cut = height * 5 // 8
    a_half, b_half = cut // 2, (height - cut) // 2
    a_all, b_all = pl.ds(0, cut), pl.ds(cut, height - cut)
    a_part = (pl.ds(0, a_half), pl.ds(a_half, a_half))
    b_part = (pl.ds(cut, b_half), pl.ds(cut + b_half, b_half))

    def zz(by):
        return lax.rem(z + by + nz, nz)

    def yy(by):
        return lax.rem(y + by + ny, ny)

    def device(y_at, z_at, core_at):
        return ((y_at * nz + z_at) * cores + core_at, col)

    z_to = (device(y, zz(1), core), device(y, zz(-1), core))
    y_to = (device(yy(1), z, core), device(yy(-1), z, core))
    sibling = device(y, z, 1 - core)
    sign = (-1, 1)

    barrier = pltpu.get_barrier_semaphore()
    for other in z_to + y_to + (sibling,):
        pl.semaphore_signal(barrier, inc=1, device_id=other, device_id_type=MESH)
    own = pltpu.make_async_copy(a2, whole.at[y, z, core], own_sem)
    own.start()
    pl.semaphore_wait(barrier, 5)

    def copy(src, dst, send_sem, recv_sem, to):
        return pltpu.make_async_remote_copy(
            src_ref=src, dst_ref=dst, send_sem=send_sem, recv_sem=recv_sem,
            device_id=to, device_id_type=MESH,
        )

    def az(d, s, part, mine=False):
        place = whole.at[y, zz(sign[d] * (s - 1)), core, part]
        return copy(a2.at[part] if mine else place, place, az_s.at[d, s], az_r.at[d, s], z_to[d])

    def az_in(d, s, part):
        place = whole.at[y, zz(sign[d] * s), core, part]
        copy(place, place, az_s.at[d, s], az_r.at[d, s], z_to[d]).wait_recv()

    def bz(d, s, part):
        place = whole.at[:, zz(sign[d] * (s - 1)), core, part]
        return copy(place, place, bz_s.at[d, s], bz_r.at[d, s], z_to[d])

    def bz_in(d, s, part):
        place = whole.at[:, zz(sign[d] * s), core, part]
        copy(place, place, bz_s.at[d, s], bz_r.at[d, s], z_to[d]).wait_recv()

    def by(d, h, y_at, part, mine=False):
        place = whole.at[y_at, z, core, part]
        return copy(a2.at[part] if mine else place, place, by_s.at[d, h], by_r.at[d, h], y_to[d])

    def ay(d, z_at, mine=False):
        place = whole.at[y, z_at, core, a_all]
        return copy(a2.at[a_all] if mine else place, place, ay_s.at[d, z_at], ay_r.at[d, z_at], y_to[d])

    def ay_in(d, z_at):
        place = whole.at[yy(sign[d]), z_at, core, a_all]
        copy(place, place, ay_s.at[d, z_at], ay_r.at[d, z_at], y_to[d]).wait_recv()

    def ah(d, y_at, z_at):
        place = whole.at[y_at, z_at, core, a_part[d]]
        return copy(place, place, ah_s.at[d, z_at], ah_r.at[d, z_at], y_to[d])

    def share(place):
        copy(place, place, sib_s, sib_r, sibling).start()

    def from_y(z_at):
        for d in range(2):
            ay_in(d, z_at)
            ah(d, yy(sign[d]), z_at).start()
            share(whole.at[yy(sign[d]), z_at, core, a_all])

    def from_y_far(z_at):
        for d in range(2):
            ah(d, yy(2), z_at).wait_recv()
        share(whole.at[yy(2), z_at, core, a_all])

    def a_step(s, last):
        for d in range(2):
            z_at = zz(sign[d] * s)
            az_in(d, s, a_all)
            az(d, s + 1, a_part[d] if last else a_all).start()
            for e in range(2):
                ay(e, z_at).start()
            share(whole.at[y, z_at, core, a_all])

    def b_step(s, last):
        for d in range(2):
            z_at = zz(sign[d] * s)
            bz_in(d, s, b_all)
            bz(d, s + 1, b_part[d] if last else b_all).start()
            share(whole.at[:, z_at, core, b_all])

    for d in range(2):
        az(d, 1, a_all, True).start()
        by(d, 0, y, b_all, True).start()
    for d in range(2):
        ay(d, z, True).start()
    for d in range(2):
        by(d, 0, yy(sign[d]), b_all).wait_recv()
        by(d, 1, yy(sign[d]), b_part[d]).start()
    own.wait()
    share(whole.at[y, z, core, a_all])
    a_step(1, False)
    for d in range(2):
        by(d, 1, yy(2), b_part[d]).wait_recv()
    for d in range(2):
        bz(d, 1, b_all).start()
    share(whole.at[:, z, core, b_all])
    from_y(z)
    a_step(2, False)
    from_y_far(z)
    for d in range(2):
        from_y(zz(sign[d]))
    b_step(1, False)

    def steady(s, carry):
        a_step(s, False)
        for d in range(2):
            from_y_far(zz(sign[d] * (s - 2)))
        for d in range(2):
            from_y(zz(sign[d] * (s - 1)))
        b_step(s - 1, False)
        return carry

    far = nz // 2
    lax.fori_loop(3, far - 1, steady, 0)
    a_step(far - 1, True)
    for d in range(2):
        from_y_far(zz(sign[d] * (far - 3)))
    for d in range(2):
        from_y(zz(sign[d] * (far - 2)))
    b_step(far - 2, False)
    for d in range(2):
        az_in(d, far, a_part[d])
    for e in range(2):
        ay(e, zz(far)).start()
    share(whole.at[y, zz(far), core, a_all])
    for d in range(2):
        from_y_far(zz(sign[d] * (far - 2)))
    for d in range(2):
        from_y(zz(sign[d] * (far - 1)))
    b_step(far - 1, True)
    from_y(zz(far))
    for d in range(2):
        from_y_far(zz(sign[d] * (far - 1)))
    for d in range(2):
        bz_in(d, far, b_part[d])
    share(whole.at[:, zz(far), core, b_all])
    from_y_far(zz(far))

    for d in range(2):
        by(d, 0, y, b_all).wait_send()
        by(d, 1, y, b_part[d]).wait_send()
        az(d, far, a_part[d]).wait_send()
        bz(d, far, b_part[d]).wait_send()

    def sent_z(s, carry):
        for d in range(2):
            az(d, s, a_all).wait_send()
            bz(d, s, b_all).wait_send()
        return carry

    lax.fori_loop(1, far, sent_z, 0)

    def sent_y(z_at, carry):
        for d in range(2):
            ay(d, z_at).wait_send()
            ah(d, y, z_at).wait_send()
        return carry

    lax.fori_loop(0, nz, sent_y, 0)
    mine, theirs = whole.at[:, :, core], whole.at[:, :, 1 - core]
    copy(mine, mine, sib_s, sib_r, sibling).wait_send()
    copy(theirs, theirs, sib_s, sib_r, sibling).wait_recv()


def gather_targets(a2_blocks):
    targets_here, block = a2_blocks.shape[0], a2_blocks.shape[1]
    height = targets_here * block
    far = nz // 2
    dma = pltpu.SemaphoreType.DMA
    zs, ys = dma((2, far + 1)), dma((2, nz))
    whole = pl.pallas_call(
        gather_kernel,
        out_shape=jax.ShapeDtypeStruct((ny, nz, cores, height, block), a2_blocks.dtype),
        in_specs=[pl.BlockSpec(memory_space=pltpu.VMEM)],
        out_specs=pl.BlockSpec(memory_space=pl.ANY),
        scratch_shapes=[dma(())] + [zs] * 4 + [dma((2, 2))] * 2 + [ys] * 4 + [dma(())] * 2,
        compiler_params=pltpu.CompilerParams(collective_id=0, has_side_effects=True),
        cost_estimate=pl.CostEstimate(flops=0, bytes_accessed=150_000_000, transcendentals=0),
    )(a2_blocks.reshape(height, block))
    return whole.reshape(ny * nz * cores * targets_here, block, block)


def local(prior, candidates, cross_link, a1_blocks, a2_blocks):
    row_blocks, per_quarter, block = prior.shape[0], prior.shape[1], prior.shape[2]
    targets_here = a2_blocks.shape[0]
    column_count = lax.axis_size("cols")
    upper_half = row_blocks // 2
    smem = pl.BlockSpec(memory_space=pltpu.SMEM)
    vmem = pl.BlockSpec(memory_space=pltpu.VMEM)
    adjacency = lax.all_gather(a1_blocks, "cols", axis=0, tiled=True)
    links = lax.all_gather(cross_link, "cols", axis=0, tiled=True)
    targets = gather_targets(a2_blocks)
    within = links % row_blocks - upper_half
    next_ids = passed_along(candidates[upper_half:], "rows", -1)
    next_prior = passed_along(prior[upper_half:], "rows", -1)
    matches = candidates[:, :, None] == next_ids[within][:, None, :]
    chosen = jnp.sum(
        jnp.where(matches, jnp.arange(per_quarter, dtype=jnp.int32)[None, None, :], 0), axis=2
    ).reshape(-1)
    found = jnp.any(matches, axis=2).astype(jnp.int32).reshape(-1)
    place = (
        candidates // (column_count * targets_here) * targets_here + candidates % targets_here
    ).reshape(-1)
    shape = jax.ShapeDtypeStruct(prior.shape, jnp.bfloat16)
    flops = 2 * row_blocks * per_quarter * block**3
    first = pl.pallas_call(
        left_kernel,
        out_shape=shape,
        in_specs=[smem, smem, smem, vmem, vmem, vmem],
        out_specs=vmem,
        cost_estimate=pl.CostEstimate(
            flops=2 * flops, bytes_accessed=4 * prior.size * 2, transcendentals=0
        ),
    )(within, chosen, found, prior, next_prior, adjacency)
    next_first = passed_along(first[upper_half:], "rows", -1)
    return pl.pallas_call(
        sweep_kernel,
        out_shape=shape,
        in_specs=[smem] * 4 + [vmem] * 5 + [pl.BlockSpec(memory_space=pl.ANY)],
        out_specs=vmem,
        scratch_shapes=[
            pltpu.VMEM((row_blocks * per_quarter, block, block), jnp.bfloat16),
            pltpu.SemaphoreType.DMA((row_blocks * per_quarter,)),
        ],
        cost_estimate=pl.CostEstimate(
            flops=6 * flops, bytes_accessed=6 * prior.size * 2, transcendentals=0
        ),
    )(within, chosen, found, place, prior, next_prior, first, next_first, adjacency, targets)


def solution(mesh):
    placed = (
        P("rows", "cols", None, None),
        P("rows", "cols"),
        P(("rows", "cols")),
        P(("rows", "cols"), None, None, None),
        P(("rows", "cols"), None, None),
    )
    return jax.shard_map(
        local, mesh=mesh, in_specs=placed, out_specs=P("rows", "cols", None, None), check_vma=False
    )
```

```python
import jax
import jax.numpy as jnp
from jax import lax
from jax.experimental import pallas as pl
from jax.experimental.pallas import tpu as pltpu
from jax.sharding import PartitionSpec as P

mixing = 0.75


def contract(a, b, dims):
    return lax.dot_general(a, b, (dims, ((), ())), preferred_element_type=jnp.float32)


MESH = pl.DeviceIdType.MESH
ny, nz, cores = 4, 16, 2


def propagate_kernel(
    meta, prior, a1, a2, out,
    whole, adjacency, next_prior, first, next_first, next_meta, col_meta,
    my_ids, next_ids, links, picks,
    own_sem, az_s, az_r, bz_s, bz_r, by_s, by_r, ay_s, ay_r, ah_s, ah_r, sib_s, sib_r,
    col_s, col_r, next_s, next_r, first_s, first_r, local_sem,
):
    rows, per, block = prior.shape[0], prior.shape[1], prior.shape[2]
    upper = rows // 2
    columns = adjacency.shape[0]
    row_share = rows // columns
    me, col = lax.axis_index("rows"), lax.axis_index("cols")
    core = lax.rem(me, cores)
    z = lax.rem(me // cores, nz)
    y = me // (cores * nz)
    height = a2.shape[0]
    cut = height * 3 // 4
    a_half, b_half = cut // 2, (height - cut) // 2
    a_all, b_all = pl.ds(0, cut), pl.ds(cut, height - cut)
    a_part = (pl.ds(0, a_half), pl.ds(a_half, a_half))
    b_part = (pl.ds(cut, b_half), pl.ds(cut + b_half, b_half))

    def zz(by):
        return lax.rem(z + by + nz, nz)

    def yy(by):
        return lax.rem(y + by + ny, ny)

    def device(y_at, z_at, core_at):
        return ((y_at * nz + z_at) * cores + core_at, col)

    z_to = (device(y, zz(1), core), device(y, zz(-1), core))
    y_to = (device(yy(1), z, core), device(yy(-1), z, core))
    sibling = device(y, z, 1 - core)
    sign = (-1, 1)
    slabs = ny * nz * cores
    before = (lax.rem(me + slabs - 1, slabs), col)
    after = (lax.rem(me + 1, slabs), col)
    col_to = tuple((me, lax.rem(col + by, columns)) for by in range(1, columns))

    barrier = pltpu.get_barrier_semaphore()
    for other in z_to + y_to + (sibling, before, after) + col_to:
        pl.semaphore_signal(barrier, inc=1, device_id=other, device_id_type=MESH)
    own = pltpu.make_async_copy(a2, whole.at[y, z, core], own_sem)
    own.start()
    own_a1 = pltpu.make_async_copy(a1, adjacency.at[col], local_sem.at[0])
    own_a1.start()
    own_links = pltpu.make_async_copy(meta, links.at[col], local_sem.at[1])
    own_links.start()
    own_ids = pltpu.make_async_copy(meta, my_ids, local_sem.at[2])
    own_ids.start()
    pl.semaphore_wait(barrier, 7 + columns - 1)

    def copy(src, dst, send_sem, recv_sem, to):
        return pltpu.make_async_remote_copy(
            src_ref=src, dst_ref=dst, send_sem=send_sem, recv_sem=recv_sem,
            device_id=to, device_id_type=MESH,
        )

    def az(d, s, part, mine=False):
        place = whole.at[y, zz(sign[d] * (s - 1)), core, part]
        return copy(a2.at[part] if mine else place, place, az_s.at[d, s], az_r.at[d, s], z_to[d])

    def az_in(d, s, part):
        place = whole.at[y, zz(sign[d] * s), core, part]
        copy(place, place, az_s.at[d, s], az_r.at[d, s], z_to[d]).wait_recv()

    def bz(d, s, part):
        place = whole.at[:, zz(sign[d] * (s - 1)), core, part]
        return copy(place, place, bz_s.at[d, s], bz_r.at[d, s], z_to[d])

    def bz_in(d, s, part):
        place = whole.at[:, zz(sign[d] * s), core, part]
        copy(place, place, bz_s.at[d, s], bz_r.at[d, s], z_to[d]).wait_recv()

    def by(d, h, y_at, part, mine=False):
        place = whole.at[y_at, z, core, part]
        return copy(a2.at[part] if mine else place, place, by_s.at[d, h], by_r.at[d, h], y_to[d])

    def ay(d, z_at, mine=False):
        place = whole.at[y, z_at, core, a_all]
        return copy(a2.at[a_all] if mine else place, place, ay_s.at[d, z_at], ay_r.at[d, z_at], y_to[d])

    def ay_in(d, z_at):
        place = whole.at[yy(sign[d]), z_at, core, a_all]
        copy(place, place, ay_s.at[d, z_at], ay_r.at[d, z_at], y_to[d]).wait_recv()

    def ah(d, y_at, z_at):
        place = whole.at[y_at, z_at, core, a_part[d]]
        return copy(place, place, ah_s.at[d, z_at], ah_r.at[d, z_at], y_to[d])

    def share(place):
        copy(place, place, sib_s, sib_r, sibling).start()

    def from_y(z_at):
        for d in range(2):
            ay_in(d, z_at)
            ah(d, yy(sign[d]), z_at).start()
            share(whole.at[yy(sign[d]), z_at, core, a_all])

    def from_y_far(z_at):
        for d in range(2):
            ah(d, yy(2), z_at).wait_recv()
        share(whole.at[yy(2), z_at, core, a_all])

    def a_step(s, last):
        for d in range(2):
            z_at = zz(sign[d] * s)
            az_in(d, s, a_all)
            az(d, s + 1, a_part[d] if last else a_all).start()
            for e in range(2):
                ay(e, z_at).start()
            share(whole.at[y, z_at, core, a_all])

    def b_step(s, last):
        for d in range(2):
            z_at = zz(sign[d] * s)
            bz_in(d, s, b_all)
            bz(d, s + 1, b_part[d] if last else b_all).start()
            share(whole.at[:, z_at, core, b_all])

    def col_a1(by, source):
        return copy(a1, adjacency.at[source], col_s.at[0, by], col_r.at[0, by], col_to[by - 1])

    def col_links(by, source):
        return copy(meta, col_meta.at[source], col_s.at[1, by], col_r.at[1, by], col_to[by - 1])

    def ids_along():
        return copy(meta, next_meta, next_s.at[0], next_r.at[0], before)

    def prior_along():
        return copy(prior.at[pl.ds(upper, upper)], next_prior, next_s.at[1], next_r.at[1], before)

    pair = upper // 4

    def first_along(part):
        here = first.at[pl.ds(upper + part * pair, pair)]
        there = next_first.at[pl.ds(part * pair, pair)]
        return copy(here, there, first_s.at[part], first_r.at[part], before)

    def left_row(i):
        owner, at = i // row_share, lax.rem(i, row_share)
        linked = lax.rem(links[owner, 1, at], upper)
        for k in range(per):
            n = i * per + k
            target = my_ids[0, n]
            chosen, found = jnp.int32(0), jnp.int32(0)
            for j in range(per):
                same = (next_ids[0, (linked + upper) * per + j] == target).astype(jnp.int32)
                chosen = chosen + same * j
                found = found + same
            picks[0, n] = linked
            chosen = lax.rem(chosen, per)
            picks[1, n] = chosen
            picks[2, n] = found
            picked = next_prior[linked, chosen]
            total = contract(adjacency[owner, at, 0], prior[i, k], ((1,), (0,)))
            cross = contract(adjacency[owner, at, 1], picked, ((1,), (0,)))
            total = total + cross * found.astype(jnp.float32)
            first[i, k] = total.astype(jnp.bfloat16)

    def sweep_row(i, carry):
        owner, at = i // row_share, lax.rem(i, row_share)
        for k in range(per):
            n = i * per + k
            name = my_ids[0, n]
            slab = lax.div(name, columns * targets)
            slab_y, slab_z = lax.div(slab, nz * cores), lax.rem(lax.div(slab, cores), nz)
            slab_core, low = lax.rem(slab, cores), lax.rem(name, targets) * 2
            target = jnp.concatenate(
                [
                    whole[slab_y, slab_z, slab_core, low],
                    whole[slab_y, slab_z, slab_core, low + 1],
                ],
                axis=0,
            )
            picked_prior = next_prior[picks[0, n], picks[1, n]]
            picked_first = next_first[picks[0, n], picks[1, n]]
            own_prior = prior[i, k]
            values = jnp.concatenate([first[i, k], picked_first], axis=0)
            base = jnp.concatenate([own_prior, picked_prior], axis=0).astype(jnp.float32)
            image = contract(values, target, ((1,), (1,)))
            swept = (mixing * image + (1.0 - mixing) * base).astype(jnp.bfloat16)
            carried = contract(swept, target, ((1,), (1,))).astype(jnp.bfloat16)
            total = contract(adjacency[owner, at, 0], carried[:block], ((1,), (0,)))
            cross = contract(adjacency[owner, at, 1], carried[block:], ((1,), (0,)))
            total = total + cross * picks[2, n].astype(jnp.float32)
            out[i, k] = (mixing * total + (1.0 - mixing) * own_prior.astype(jnp.float32)).astype(
                jnp.bfloat16
            )
        return carry

    def left_rows(s):
        for i in range(pair):
            left_row(upper + (s - 3) * pair + i)
        for i in range(pair):
            left_row((s - 3) * pair + i)

    targets = whole.shape[3] // 2
    ids_along().start()
    for by_col in range(1, columns):
        col_links(by_col, col).start()
        col_a1(by_col, col).start()
    for d in range(2):
        az(d, 1, a_all, True).start()
        by(d, 0, y, b_all, True).start()
    for d in range(2):
        ay(d, z, True).start()
    prior_along().start()
    for d in range(2):
        by(d, 0, yy(sign[d]), b_all).wait_recv()
        by(d, 1, yy(sign[d]), b_part[d]).start()
    own.wait()
    share(whole.at[y, z, core, a_all])
    a_step(1, False)
    for d in range(2):
        by(d, 1, yy(2), b_part[d]).wait_recv()
    for d in range(2):
        bz(d, 1, b_all).start()
    share(whole.at[:, z, core, b_all])
    from_y(z)
    a_step(2, False)
    from_y_far(z)
    for d in range(2):
        from_y(zz(sign[d]))
    b_step(1, False)

    own_ids.wait()
    own_links.wait()
    own_a1.wait()
    ids_along().wait_recv()
    to_smem = pltpu.make_async_copy(next_meta, next_ids, local_sem.at[2])
    to_smem.start()
    for by_col in range(1, columns):
        source = lax.rem(col + columns - by_col, columns)
        col_links(by_col, source).wait_recv()
        moved = pltpu.make_async_copy(col_meta.at[source], links.at[source], local_sem.at[1])
        moved.start()
        moved.wait()
        col_a1(by_col, source).wait_recv()
    to_smem.wait()
    prior_along().wait_recv()

    def steady(s, carry):
        a_step(s, False)
        if not isinstance(s, int):
            first_along(s - 4).start()
        for d in range(2):
            from_y_far(zz(sign[d] * (s - 2)))
        for d in range(2):
            from_y(zz(sign[d] * (s - 1)))
        b_step(s - 1, False)
        left_rows(s)
        return carry

    far = nz // 2
    steady(3, 0)
    lax.fori_loop(4, far - 1, steady, 0)
    a_step(far - 1, True)
    first_along(3).start()
    for d in range(2):
        from_y_far(zz(sign[d] * (far - 3)))
    for d in range(2):
        from_y(zz(sign[d] * (far - 2)))
    b_step(far - 2, False)
    for d in range(2):
        az_in(d, far, a_part[d])
    for e in range(2):
        ay(e, zz(far)).start()
    share(whole.at[y, zz(far), core, a_all])
    for d in range(2):
        from_y_far(zz(sign[d] * (far - 2)))
    for d in range(2):
        from_y(zz(sign[d] * (far - 1)))
    b_step(far - 1, True)
    from_y(zz(far))
    for d in range(2):
        from_y_far(zz(sign[d] * (far - 1)))
    for d in range(2):
        bz_in(d, far, b_part[d])
    share(whole.at[:, zz(far), core, b_all])
    from_y_far(zz(far))

    for d in range(2):
        by(d, 0, y, b_all).wait_send()
        by(d, 1, y, b_part[d]).wait_send()
        az(d, far, a_part[d]).wait_send()
        bz(d, far, b_part[d]).wait_send()

    def sent_z(s, carry):
        for d in range(2):
            az(d, s, a_all).wait_send()
            bz(d, s, b_all).wait_send()
        return carry

    lax.fori_loop(1, far, sent_z, 0)

    def sent_y(z_at, carry):
        for d in range(2):
            ay(d, z_at).wait_send()
            ah(d, y, z_at).wait_send()
        return carry

    lax.fori_loop(0, nz, sent_y, 0)
    mine, theirs = whole.at[:, :, core], whole.at[:, :, 1 - core]
    copy(mine, mine, sib_s, sib_r, sibling).wait_send()
    copy(theirs, theirs, sib_s, sib_r, sibling).wait_recv()
    ids_along().wait_send()
    prior_along().wait_send()
    for by_col in range(1, columns):
        col_links(by_col, col).wait_send()
        col_a1(by_col, col).wait_send()
    for part in range(4):
        first_along(part).wait_send()
        first_along(part).wait_recv()
    lax.fori_loop(0, rows, sweep_row, 0)


def local(prior, candidates, cross_link, a1_blocks, a2_blocks):
    rows, per, block = prior.shape[0], prior.shape[1], prior.shape[2]
    columns = lax.axis_size("cols")
    targets_here = a2_blocks.shape[0]
    upper = rows // 2
    pieces = a2_blocks.reshape(2 * targets_here, block // 2, block)
    far = nz // 2
    lanes = 128
    ids = jnp.pad(candidates.reshape(1, -1), ((0, 0), (0, lanes - candidates.size)))
    names = jnp.pad(cross_link.reshape(1, -1), ((0, 6), (0, lanes - cross_link.size)))
    meta = jnp.concatenate([ids, names], axis=0)
    tile = meta.shape
    dma = pltpu.SemaphoreType.DMA
    zs, ys = dma((2, far + 1)), dma((2, nz))
    vmem = pl.BlockSpec(memory_space=pltpu.VMEM)
    half = (upper,) + prior.shape[1:]
    return pl.pallas_call(
        propagate_kernel,
        out_shape=jax.ShapeDtypeStruct(prior.shape, prior.dtype),
        in_specs=[vmem] * 4,
        out_specs=vmem,
        scratch_shapes=[
            pltpu.VMEM((ny, nz, cores) + pieces.shape, jnp.bfloat16),
            pltpu.VMEM((columns,) + a1_blocks.shape, jnp.bfloat16),
            pltpu.VMEM(half, jnp.bfloat16),
            pltpu.VMEM(prior.shape, jnp.bfloat16),
            pltpu.VMEM(half, jnp.bfloat16),
            pltpu.VMEM(tile, jnp.int32),
            pltpu.VMEM((columns,) + tile, jnp.int32),
            pltpu.SMEM(tile, jnp.int32),
            pltpu.SMEM(tile, jnp.int32),
            pltpu.SMEM((columns,) + tile, jnp.int32),
            pltpu.SMEM(tile, jnp.int32),
        ]
        + [dma(())]
        + [zs] * 4
        + [dma((2, 2))] * 2
        + [ys] * 4
        + [dma(())] * 2
        + [dma((2, columns))] * 2
        + [dma((2,))] * 2
        + [dma((4,))] * 2
        + [dma((3,))],
        compiler_params=pltpu.CompilerParams(collective_id=0, has_side_effects=True),
    )(meta, prior, a1_blocks, pieces)


def solution(mesh):
    placed = (
        P("rows", "cols", None, None),
        P("rows", "cols"),
        P(("rows", "cols")),
        P(("rows", "cols"), None, None, None),
        P(("rows", "cols"), None, None),
    )
    return jax.shard_map(
        local, mesh=mesh, in_specs=placed, out_specs=P("rows", "cols", None, None), check_vma=False
    )
```

```python
import jax
import jax.numpy as jnp
from jax import lax
from jax.experimental import pallas as pl
from jax.experimental.pallas import tpu as pltpu
from jax.sharding import PartitionSpec as P

mixing = 0.75


def contract(a, b, dims):
    return lax.dot_general(a, b, (dims, ((), ())), preferred_element_type=jnp.float32)


MESH = pl.DeviceIdType.MESH
ny, nz, cores = 4, 16, 2
hops = (9, 6)


def propagate_kernel(
    meta, prior, a1, a2, out,
    whole, adjacency, next_prior, first, next_first, next_meta, col_meta,
    my_ids, next_ids, links, picks,
    own_sem, az_s, az_r, bz_s, bz_r, by_s, by_r, ay_s, ay_r, ah_s, ah_r, sib_s, sib_r,
    col_s, col_r, next_s, next_r, first_s, first_r, local_sem,
):
    rows, per, block = prior.shape[0], prior.shape[1], prior.shape[2]
    upper = rows // 2
    columns = adjacency.shape[0]
    row_share = rows // columns
    me, col = lax.axis_index("rows"), lax.axis_index("cols")
    core = lax.rem(me, cores)
    z = lax.rem(me // cores, nz)
    y = me // (cores * nz)
    height = a2.shape[0]
    cut = height * 3 // 4
    a_half, b_half = cut // 2, (height - cut) // 2
    a_all, b_all = pl.ds(0, cut), pl.ds(cut, height - cut)
    a_part = (pl.ds(0, a_half), pl.ds(a_half, a_half))
    b_part = (pl.ds(cut, b_half), pl.ds(cut + b_half, b_half))

    def zz(by):
        return lax.rem(z + by + nz, nz)

    def yy(by):
        return lax.rem(y + by + ny, ny)

    def device(y_at, z_at, core_at):
        return ((y_at * nz + z_at) * cores + core_at, col)

    z_to = (device(y, zz(1), core), device(y, zz(-1), core))
    y_to = (device(yy(1), z, core), device(yy(-1), z, core))
    sibling = device(y, z, 1 - core)
    sign = (-1, 1)
    slabs = ny * nz * cores
    before = (lax.rem(me + slabs - 1, slabs), col)
    after = (lax.rem(me + 1, slabs), col)
    col_to = tuple((me, lax.rem(col + by, columns)) for by in range(1, columns))

    barrier = pltpu.get_barrier_semaphore()
    for other in z_to + y_to + (sibling, before, after) + col_to:
        pl.semaphore_signal(barrier, inc=1, device_id=other, device_id_type=MESH)
    own = pltpu.make_async_copy(a2, whole.at[y, z, core], own_sem)
    own.start()
    own_a1 = pltpu.make_async_copy(a1, adjacency.at[col], local_sem.at[0])
    own_a1.start()
    own_links = pltpu.make_async_copy(meta, links.at[col], local_sem.at[1])
    own_links.start()
    own_ids = pltpu.make_async_copy(meta, my_ids, local_sem.at[2])
    own_ids.start()
    pl.semaphore_wait(barrier, 7 + columns - 1)

    def copy(src, dst, send_sem, recv_sem, to):
        return pltpu.make_async_remote_copy(
            src_ref=src, dst_ref=dst, send_sem=send_sem, recv_sem=recv_sem,
            device_id=to, device_id_type=MESH,
        )

    def az(d, s, part, mine=False):
        place = whole.at[y, zz(sign[d] * (s - 1)), core, part]
        return copy(a2.at[part] if mine else place, place, az_s.at[d, s], az_r.at[d, s], z_to[d])

    def az_in(d, s, part):
        place = whole.at[y, zz(sign[d] * s), core, part]
        copy(place, place, az_s.at[d, s], az_r.at[d, s], z_to[d]).wait_recv()

    def bz(d, s, part):
        place = whole.at[:, zz(sign[d] * (s - 1)), core, part]
        return copy(place, place, bz_s.at[d, s], bz_r.at[d, s], z_to[d])

    def bz_in(d, s, part):
        place = whole.at[:, zz(sign[d] * s), core, part]
        copy(place, place, bz_s.at[d, s], bz_r.at[d, s], z_to[d]).wait_recv()

    def by(d, h, y_at, part, mine=False):
        place = whole.at[y_at, z, core, part]
        return copy(a2.at[part] if mine else place, place, by_s.at[d, h], by_r.at[d, h], y_to[d])

    def ay(d, z_at, mine=False):
        place = whole.at[y, z_at, core, a_all]
        return copy(a2.at[a_all] if mine else place, place, ay_s.at[d, z_at], ay_r.at[d, z_at], y_to[d])

    def ay_in(d, z_at):
        place = whole.at[yy(sign[d]), z_at, core, a_all]
        copy(place, place, ay_s.at[d, z_at], ay_r.at[d, z_at], y_to[d]).wait_recv()

    def ah(d, y_at, z_at):
        place = whole.at[y_at, z_at, core, a_part[d]]
        return copy(place, place, ah_s.at[d, z_at], ah_r.at[d, z_at], y_to[d])

    def share(place):
        copy(place, place, sib_s, sib_r, sibling).start()

    def from_y(z_at):
        for d in range(2):
            ay_in(d, z_at)
            ah(d, yy(sign[d]), z_at).start()
            share(whole.at[yy(sign[d]), z_at, core, a_all])

    def from_y_far(z_at):
        for d in range(2):
            ah(d, yy(2), z_at).wait_recv()
        share(whole.at[yy(2), z_at, core, a_all])

    def going(s):
        return [d for d in range(2) if s <= hops[d]]

    def sources(s):
        return [zz(sign[d] * s) for d in going(s)] if s else [z]

    def a_step(s):
        for d in going(s):
            z_at = zz(sign[d] * s)
            az_in(d, s, a_all)
            if s < hops[d]:
                az(d, s + 1, a_all).start()
            for e in range(2):
                ay(e, z_at).start()
            share(whole.at[y, z_at, core, a_all])

    def b_step(s):
        for d in going(s):
            z_at = zz(sign[d] * s)
            bz_in(d, s, b_all)
            if s < hops[d]:
                bz(d, s + 1, b_all).start()
            share(whole.at[:, z_at, core, b_all])

    def col_a1(by, source):
        return copy(a1, adjacency.at[source], col_s.at[0, by], col_r.at[0, by], col_to[by - 1])

    def col_links(by, source):
        return copy(meta, col_meta.at[source], col_s.at[1, by], col_r.at[1, by], col_to[by - 1])

    def ids_along():
        return copy(meta, next_meta, next_s.at[0], next_r.at[0], before)

    def prior_along():
        return copy(prior.at[pl.ds(upper, upper)], next_prior, next_s.at[1], next_r.at[1], before)

    pair = upper // 4

    def first_along(part):
        here = first.at[pl.ds(upper + part * pair, pair)]
        there = next_first.at[pl.ds(part * pair, pair)]
        return copy(here, there, first_s.at[part], first_r.at[part], before)

    def left_row(i):
        owner, at = i // row_share, lax.rem(i, row_share)
        linked = lax.rem(links[owner, 1, at], upper)
        for k in range(per):
            n = i * per + k
            target = my_ids[0, n]
            chosen, found = jnp.int32(0), jnp.int32(0)
            for j in range(per):
                same = (next_ids[0, (linked + upper) * per + j] == target).astype(jnp.int32)
                chosen = chosen + same * j
                found = found + same
            picks[0, n] = linked
            chosen = lax.rem(chosen, per)
            picks[1, n] = chosen
            picks[2, n] = found
            picked = next_prior[linked, chosen]
            total = contract(adjacency[owner, at, 0], prior[i, k], ((1,), (0,)))
            cross = contract(adjacency[owner, at, 1], picked, ((1,), (0,)))
            total = total + cross * found.astype(jnp.float32)
            first[i, k] = total.astype(jnp.bfloat16)

    def target_of(n):
        name = my_ids[0, n]
        slab = lax.div(name, columns * targets)
        slab_y, slab_z = lax.div(slab, nz * cores), lax.rem(lax.div(slab, cores), nz)
        slab_core, low = lax.rem(slab, cores), lax.rem(name, targets) * 2
        upper_part = whole[slab_y, slab_z, slab_core, low]
        return jnp.concatenate([upper_part, whole[slab_y, slab_z, slab_core, low + 1]], axis=0)

    def square(a, b, c, d):
        top, bottom = jnp.concatenate([a, b], axis=1), jnp.concatenate([c, d], axis=1)
        return jnp.concatenate([top, bottom], axis=0)

    def sweep_row(i, carry):
        owner, at = i // row_share, lax.rem(i, row_share)
        weights = jnp.concatenate([adjacency[owner, at, 0], adjacency[owner, at, 1]], axis=1)
        for k in range(0, per, 2):
            n, m = i * per + k, i * per + k + 1
            one, two = target_of(n), target_of(m)
            zero = jnp.zeros_like(one)
            both = square(one, zero, zero, two)
            values = square(
                first[i, k],
                first[i, k + 1],
                next_first[picks[0, n], picks[1, n]],
                next_first[picks[0, m], picks[1, m]],
            )
            base = square(
                prior[i, k],
                prior[i, k + 1],
                next_prior[picks[0, n], picks[1, n]],
                next_prior[picks[0, m], picks[1, m]],
            ).astype(jnp.float32)
            image = contract(values, both, ((1,), (1,)))
            swept = (mixing * image + (1.0 - mixing) * base).astype(jnp.bfloat16)
            carried = contract(swept, both, ((1,), (1,)))
            stacked = square(
                carried[:block, :block],
                carried[:block, block:],
                carried[block:, :block] * picks[2, n].astype(jnp.float32),
                carried[block:, block:] * picks[2, m].astype(jnp.float32),
            ).astype(jnp.bfloat16)
            total = contract(weights, stacked, ((1,), (0,)))
            mixed = (mixing * total + (1.0 - mixing) * base[:block]).astype(jnp.bfloat16)
            out[i, k] = mixed[:, :block]
            out[i, k + 1] = mixed[:, block:]
        return carry

    def left_rows(s):
        def one(i, carry):
            left_row(upper + (s - 3) * pair + i)
            left_row((s - 3) * pair + i)
            return carry

        lax.fori_loop(0, pair, one, 0)

    targets = whole.shape[3] // 2
    ids_along().start()
    for by_col in range(1, columns):
        col_links(by_col, col).start()
        col_a1(by_col, col).start()
    for d in range(2):
        az(d, 1, a_all, True).start()
        by(d, 0, y, b_all, True).start()
    for d in range(2):
        ay(d, z, True).start()
    prior_along().start()
    for d in range(2):
        by(d, 0, yy(sign[d]), b_all).wait_recv()
        by(d, 1, yy(sign[d]), b_part[d]).start()
    own.wait()
    share(whole.at[y, z, core, a_all])
    a_step(1)
    for d in range(2):
        by(d, 1, yy(2), b_part[d]).wait_recv()
    for d in range(2):
        bz(d, 1, b_all).start()
    share(whole.at[:, z, core, b_all])
    from_y(z)
    a_step(2)
    b_step(1)
    from_y_far(z)
    for z_at in sources(1):
        from_y(z_at)
    own_ids.wait()
    own_links.wait()
    own_a1.wait()
    ids_along().wait_recv()
    to_smem = pltpu.make_async_copy(next_meta, next_ids, local_sem.at[2])
    to_smem.start()
    for by_col in range(1, columns):
        source = lax.rem(col + columns - by_col, columns)
        col_links(by_col, source).wait_recv()
        moved = pltpu.make_async_copy(col_meta.at[source], links.at[source], local_sem.at[1])
        moved.start()
        moved.wait()
        col_a1(by_col, source).wait_recv()
    to_smem.wait()
    prior_along().wait_recv()

    longest = max(hops)
    for s in range(3, longest + 2):
        a_step(s)
        b_step(s - 1)
        if 4 <= s < 8:
            first_along(s - 4).start()
        for z_at in sources(s - 2):
            from_y_far(z_at)
        for z_at in sources(s - 1):
            from_y(z_at)
        if s < 7:
            left_rows(s)
    for z_at in sources(longest):
        from_y_far(z_at)
    for d in range(2):
        by(d, 0, y, b_all).wait_send()
        by(d, 1, y, b_part[d]).wait_send()

        def sent_z(s, carry, d=d):
            az(d, s, a_all).wait_send()
            bz(d, s, b_all).wait_send()
            return carry

        lax.fori_loop(1, hops[d] + 1, sent_z, 0)

    def sent_y(z_at, carry):
        for d in range(2):
            ay(d, z_at).wait_send()
            ah(d, y, z_at).wait_send()
        return carry

    lax.fori_loop(0, nz, sent_y, 0)
    mine, theirs = whole.at[:, :, core], whole.at[:, :, 1 - core]
    copy(mine, mine, sib_s, sib_r, sibling).wait_send()
    copy(theirs, theirs, sib_s, sib_r, sibling).wait_recv()
    ids_along().wait_send()
    prior_along().wait_send()
    for by_col in range(1, columns):
        col_links(by_col, col).wait_send()
        col_a1(by_col, col).wait_send()
    for part in range(4):
        first_along(part).wait_send()
        first_along(part).wait_recv()
    lax.fori_loop(0, rows, sweep_row, 0)


def local(prior, candidates, cross_link, a1_blocks, a2_blocks):
    rows, per, block = prior.shape[0], prior.shape[1], prior.shape[2]
    columns = lax.axis_size("cols")
    targets_here = a2_blocks.shape[0]
    upper = rows // 2
    pieces = a2_blocks.reshape(2 * targets_here, block // 2, block)
    lanes = 128
    ids = jnp.pad(candidates.reshape(1, -1), ((0, 0), (0, lanes - candidates.size)))
    names = jnp.pad(cross_link.reshape(1, -1), ((0, 6), (0, lanes - cross_link.size)))
    meta = jnp.concatenate([ids, names], axis=0)
    tile = meta.shape
    dma = pltpu.SemaphoreType.DMA
    zs, ys = dma((2, max(hops) + 1)), dma((2, nz))
    vmem = pl.BlockSpec(memory_space=pltpu.VMEM)
    half = (upper,) + prior.shape[1:]
    return pl.pallas_call(
        propagate_kernel,
        out_shape=jax.ShapeDtypeStruct(prior.shape, prior.dtype),
        in_specs=[vmem] * 4,
        out_specs=vmem,
        scratch_shapes=[
            pltpu.VMEM((ny, nz, cores) + pieces.shape, jnp.bfloat16),
            pltpu.VMEM((columns,) + a1_blocks.shape, jnp.bfloat16),
            pltpu.VMEM(half, jnp.bfloat16),
            pltpu.VMEM(prior.shape, jnp.bfloat16),
            pltpu.VMEM(half, jnp.bfloat16),
            pltpu.VMEM(tile, jnp.int32),
            pltpu.VMEM((columns,) + tile, jnp.int32),
            pltpu.SMEM(tile, jnp.int32),
            pltpu.SMEM(tile, jnp.int32),
            pltpu.SMEM((columns,) + tile, jnp.int32),
            pltpu.SMEM(tile, jnp.int32),
        ]
        + [dma(())]
        + [zs] * 4
        + [dma((2, 2))] * 2
        + [ys] * 4
        + [dma(())] * 2
        + [dma((2, columns))] * 2
        + [dma((2,))] * 2
        + [dma((4,))] * 2
        + [dma((3,))],
        compiler_params=pltpu.CompilerParams(collective_id=0, has_side_effects=True),
    )(meta, prior, a1_blocks, pieces)


def solution(mesh):
    placed = (
        P("rows", "cols", None, None),
        P("rows", "cols"),
        P(("rows", "cols")),
        P(("rows", "cols"), None, None, None),
        P(("rows", "cols"), None, None),
    )
    return jax.shard_map(
        local, mesh=mesh, in_specs=placed, out_specs=P("rows", "cols", None, None), check_vma=False
    )
```

```python
import jax
import jax.numpy as jnp
from jax import lax
from jax.experimental import pallas as pl
from jax.experimental.pallas import tpu as pltpu
from jax.sharding import PartitionSpec as P

mixing = 0.75


def contract(a, b, dims):
    return lax.dot_general(a, b, (dims, ((), ())), preferred_element_type=jnp.float32)


MESH = pl.DeviceIdType.MESH
ny, nz, cores = 4, 16, 2
hops = (9, 6)


def propagate_kernel(
    meta, prior, a1, a2, out,
    whole, adjacency, next_prior, first, next_first, next_meta, col_meta,
    my_ids, next_ids, links, picks,
    own_sem, az_s, az_r, bz_s, bz_r, by_s, by_r, ay_s, ay_r, ah_s, ah_r, sib_s, sib_r,
    col_s, col_r, next_s, next_r, first_s, first_r, local_sem,
):
    rows, per, block = prior.shape[0], prior.shape[1], prior.shape[2]
    upper = rows // 2
    columns = adjacency.shape[0]
    row_share = rows // columns
    me, col = lax.axis_index("rows"), lax.axis_index("cols")
    core = lax.rem(me, cores)
    z = lax.rem(me // cores, nz)
    y = me // (cores * nz)
    height = a2.shape[0]
    cut = height * 3 // 4
    a_half, b_half = cut // 2, (height - cut) // 2
    a_all, b_all = pl.ds(0, cut), pl.ds(cut, height - cut)
    a_part = (pl.ds(0, a_half), pl.ds(a_half, a_half))
    b_part = (pl.ds(cut, b_half), pl.ds(cut + b_half, b_half))

    def zz(by):
        return lax.rem(z + by + nz, nz)

    def yy(by):
        return lax.rem(y + by + ny, ny)

    def device(y_at, z_at, core_at):
        return ((y_at * nz + z_at) * cores + core_at, col)

    z_to = (device(y, zz(1), core), device(y, zz(-1), core))
    y_to = (device(yy(1), z, core), device(yy(-1), z, core))
    sibling = device(y, z, 1 - core)
    sign = (-1, 1)
    slabs = ny * nz * cores
    before = (lax.rem(me + slabs - 1, slabs), col)
    after = (lax.rem(me + 1, slabs), col)
    col_to = tuple((me, lax.rem(col + by, columns)) for by in range(1, columns))

    barrier = pltpu.get_barrier_semaphore()
    for other in z_to + y_to + (sibling, before, after) + col_to:
        pl.semaphore_signal(barrier, inc=1, device_id=other, device_id_type=MESH)
    own = pltpu.make_async_copy(a2, whole.at[y, z, core], own_sem)
    own.start()
    own_a1 = pltpu.make_async_copy(a1, adjacency.at[col], local_sem.at[0])
    own_a1.start()
    own_links = pltpu.make_async_copy(meta, links.at[col], local_sem.at[1])
    own_links.start()
    own_ids = pltpu.make_async_copy(meta, my_ids, local_sem.at[2])
    own_ids.start()
    pl.semaphore_wait(barrier, 7 + columns - 1)

    def copy(src, dst, send_sem, recv_sem, to):
        return pltpu.make_async_remote_copy(
            src_ref=src, dst_ref=dst, send_sem=send_sem, recv_sem=recv_sem,
            device_id=to, device_id_type=MESH,
        )

    def az(d, s, part, mine=False):
        place = whole.at[y, zz(sign[d] * (s - 1)), core, part]
        return copy(a2.at[part] if mine else place, place, az_s.at[d, s], az_r.at[d, s], z_to[d])

    def az_in(d, s, part):
        place = whole.at[y, zz(sign[d] * s), core, part]
        copy(place, place, az_s.at[d, s], az_r.at[d, s], z_to[d]).wait_recv()

    def bz(d, s, part):
        place = whole.at[:, zz(sign[d] * (s - 1)), core, part]
        return copy(place, place, bz_s.at[d, s], bz_r.at[d, s], z_to[d])

    def bz_in(d, s, part):
        place = whole.at[:, zz(sign[d] * s), core, part]
        copy(place, place, bz_s.at[d, s], bz_r.at[d, s], z_to[d]).wait_recv()

    def by(d, h, y_at, part, mine=False):
        place = whole.at[y_at, z, core, part]
        return copy(a2.at[part] if mine else place, place, by_s.at[d, h], by_r.at[d, h], y_to[d])

    def ay(d, z_at, mine=False):
        place = whole.at[y, z_at, core, a_all]
        return copy(a2.at[a_all] if mine else place, place, ay_s.at[d, z_at], ay_r.at[d, z_at], y_to[d])

    def ay_in(d, z_at):
        place = whole.at[yy(sign[d]), z_at, core, a_all]
        copy(place, place, ay_s.at[d, z_at], ay_r.at[d, z_at], y_to[d]).wait_recv()

    def ah(d, y_at, z_at):
        place = whole.at[y_at, z_at, core, a_part[d]]
        return copy(place, place, ah_s.at[d, z_at], ah_r.at[d, z_at], y_to[d])

    def share(place):
        copy(place, place, sib_s, sib_r, sibling).start()

    def from_y(z_at):
        for d in range(2):
            ay_in(d, z_at)
            ah(d, yy(sign[d]), z_at).start()
            share(whole.at[yy(sign[d]), z_at, core, a_all])

    def from_y_far(z_at):
        for d in range(2):
            ah(d, yy(2), z_at).wait_recv()
        share(whole.at[yy(2), z_at, core, a_all])

    def going(s):
        return [d for d in range(2) if s <= hops[d]]

    def sources(s):
        return [zz(sign[d] * s) for d in going(s)] if s else [z]

    def a_step(s):
        for d in going(s):
            z_at = zz(sign[d] * s)
            az_in(d, s, a_all)
            if s < hops[d]:
                az(d, s + 1, a_all).start()
            for e in range(2):
                ay(e, z_at).start()
            share(whole.at[y, z_at, core, a_all])

    def b_step(s):
        for d in going(s):
            z_at = zz(sign[d] * s)
            bz_in(d, s, b_all)
            if s < hops[d]:
                bz(d, s + 1, b_all).start()
            share(whole.at[:, z_at, core, b_all])

    def col_a1(by, source):
        return copy(a1, adjacency.at[source], col_s.at[0, by], col_r.at[0, by], col_to[by - 1])

    def col_links(by, source):
        return copy(meta, col_meta.at[source], col_s.at[1, by], col_r.at[1, by], col_to[by - 1])

    def ids_along():
        return copy(meta, next_meta, next_s.at[0], next_r.at[0], before)

    def prior_along():
        return copy(prior.at[pl.ds(upper, upper)], next_prior, next_s.at[1], next_r.at[1], before)

    pair = upper // 4

    def first_along(part):
        here = first.at[pl.ds(upper + part * pair, pair)]
        there = next_first.at[pl.ds(part * pair, pair)]
        return copy(here, there, first_s.at[part], first_r.at[part], before)

    def left_row(i):
        owner, at = i // row_share, lax.rem(i, row_share)
        linked = lax.rem(links[owner, 1, at], upper)
        for k in range(per):
            n = i * per + k
            target = my_ids[0, n]
            chosen, found = jnp.int32(0), jnp.int32(0)
            for j in range(per):
                same = (next_ids[0, (linked + upper) * per + j] == target).astype(jnp.int32)
                chosen = chosen + same * j
                found = found + same
            picks[0, n] = linked
            chosen = lax.rem(chosen, per)
            picks[1, n] = chosen
            picks[2, n] = found
            picked = next_prior[linked, chosen]
            total = contract(adjacency[owner, at, 0], prior[i, k], ((1,), (0,)))
            cross = contract(adjacency[owner, at, 1], picked, ((1,), (0,)))
            total = total + cross * found.astype(jnp.float32)
            first[i, k] = total.astype(jnp.bfloat16)

    def target_of(n):
        name = my_ids[0, n]
        slab = lax.div(name, columns * targets)
        slab_y, slab_z = lax.div(slab, nz * cores), lax.rem(lax.div(slab, cores), nz)
        slab_core, low = lax.rem(slab, cores), lax.rem(name, targets) * 2
        upper_part = whole[slab_y, slab_z, slab_core, low]
        return jnp.concatenate([upper_part, whole[slab_y, slab_z, slab_core, low + 1]], axis=0)

    def square(a, b, c, d):
        top, bottom = jnp.concatenate([a, b], axis=1), jnp.concatenate([c, d], axis=1)
        return jnp.concatenate([top, bottom], axis=0)

    def sweep_row(i, carry):
        owner, at = i // row_share, lax.rem(i, row_share)
        weights = jnp.concatenate([adjacency[owner, at, 0], adjacency[owner, at, 1]], axis=1)
        for k in range(0, per, 2):
            n, m = i * per + k, i * per + k + 1
            one, two = target_of(n), target_of(m)
            zero = jnp.zeros_like(one)
            both = square(one, zero, zero, two)
            values = square(
                first[i, k],
                first[i, k + 1],
                next_first[picks[0, n], picks[1, n]],
                next_first[picks[0, m], picks[1, m]],
            )
            base = square(
                prior[i, k],
                prior[i, k + 1],
                next_prior[picks[0, n], picks[1, n]],
                next_prior[picks[0, m], picks[1, m]],
            ).astype(jnp.float32)
            image = contract(values, both, ((1,), (1,)))
            swept = (mixing * image + (1.0 - mixing) * base).astype(jnp.bfloat16)
            carried = contract(swept, both, ((1,), (1,)))
            stacked = square(
                carried[:block, :block],
                carried[:block, block:],
                carried[block:, :block] * picks[2, n].astype(jnp.float32),
                carried[block:, block:] * picks[2, m].astype(jnp.float32),
            ).astype(jnp.bfloat16)
            total = contract(weights, stacked, ((1,), (0,)))
            mixed = (mixing * total + (1.0 - mixing) * base[:block]).astype(jnp.bfloat16)
            out[i, k] = mixed[:, :block]
            out[i, k + 1] = mixed[:, block:]
        return carry

    def left_rows(s):
        def one(i, carry):
            left_row(upper + s * pair + i)
            left_row(s * pair + i)
            return carry

        lax.fori_loop(0, pair, one, 0)

    targets = whole.shape[3] // 2
    ids_along().start()
    for by_col in range(1, columns):
        col_links(by_col, col).start()
        col_a1(by_col, col).start()
    for d in range(2):
        az(d, 1, a_all, True).start()
        by(d, 0, y, b_all, True).start()
    for d in range(2):
        ay(d, z, True).start()
    prior_along().start()
    for d in range(2):
        by(d, 0, yy(sign[d]), b_all).wait_recv()
        by(d, 1, yy(sign[d]), b_part[d]).start()
    own.wait()
    share(whole.at[y, z, core, a_all])
    a_step(1)
    for d in range(2):
        by(d, 1, yy(2), b_part[d]).wait_recv()
    for d in range(2):
        bz(d, 1, b_all).start()
    share(whole.at[:, z, core, b_all])
    def ready():
        own_ids.wait()
        own_links.wait()
        own_a1.wait()
        ids_along().wait_recv()
        to_smem = pltpu.make_async_copy(next_meta, next_ids, local_sem.at[2])
        to_smem.start()
        for by_col in range(1, columns):
            source = lax.rem(col + columns - by_col, columns)
            col_links(by_col, source).wait_recv()
            moved = pltpu.make_async_copy(col_meta.at[source], links.at[source], local_sem.at[1])
            moved.start()
            moved.wait()
            col_a1(by_col, source).wait_recv()
        to_smem.wait()
        prior_along().wait_recv()

    longest = max(hops)
    for s in range(2, longest + 5):
        a_step(s)
        b_step(s - 1)
        if 6 <= s < 10:
            first_along(s - 6).start()
        for z_at in sources(s - 2):
            from_y(z_at)
        if s >= 4:
            for z_at in sources(s - 4):
                from_y_far(z_at)
        if s == 5:
            ready()
        if 5 <= s < 9:
            left_rows(s - 5)
    for d in range(2):
        by(d, 0, y, b_all).wait_send()
        by(d, 1, y, b_part[d]).wait_send()

        def sent_z(s, carry, d=d):
            az(d, s, a_all).wait_send()
            bz(d, s, b_all).wait_send()
            return carry

        lax.fori_loop(1, hops[d] + 1, sent_z, 0)

    def sent_y(z_at, carry):
        for d in range(2):
            ay(d, z_at).wait_send()
            ah(d, y, z_at).wait_send()
        return carry

    lax.fori_loop(0, nz, sent_y, 0)
    mine, theirs = whole.at[:, :, core], whole.at[:, :, 1 - core]
    copy(mine, mine, sib_s, sib_r, sibling).wait_send()
    copy(theirs, theirs, sib_s, sib_r, sibling).wait_recv()
    ids_along().wait_send()
    prior_along().wait_send()
    for by_col in range(1, columns):
        col_links(by_col, col).wait_send()
        col_a1(by_col, col).wait_send()
    for part in range(4):
        first_along(part).wait_send()
        first_along(part).wait_recv()
    lax.fori_loop(0, rows, sweep_row, 0)


def local(prior, candidates, cross_link, a1_blocks, a2_blocks):
    rows, per, block = prior.shape[0], prior.shape[1], prior.shape[2]
    columns = lax.axis_size("cols")
    targets_here = a2_blocks.shape[0]
    upper = rows // 2
    pieces = a2_blocks.reshape(2 * targets_here, block // 2, block)
    lanes = 128
    ids = jnp.pad(candidates.reshape(1, -1), ((0, 0), (0, lanes - candidates.size)))
    names = jnp.pad(cross_link.reshape(1, -1), ((0, 6), (0, lanes - cross_link.size)))
    meta = jnp.concatenate([ids, names], axis=0)
    tile = meta.shape
    dma = pltpu.SemaphoreType.DMA
    zs, ys = dma((2, max(hops) + 1)), dma((2, nz))
    vmem = pl.BlockSpec(memory_space=pltpu.VMEM)
    half = (upper,) + prior.shape[1:]
    return pl.pallas_call(
        propagate_kernel,
        out_shape=jax.ShapeDtypeStruct(prior.shape, prior.dtype),
        in_specs=[vmem] * 4,
        out_specs=vmem,
        scratch_shapes=[
            pltpu.VMEM((ny, nz, cores) + pieces.shape, jnp.bfloat16),
            pltpu.VMEM((columns,) + a1_blocks.shape, jnp.bfloat16),
            pltpu.VMEM(half, jnp.bfloat16),
            pltpu.VMEM(prior.shape, jnp.bfloat16),
            pltpu.VMEM(half, jnp.bfloat16),
            pltpu.VMEM(tile, jnp.int32),
            pltpu.VMEM((columns,) + tile, jnp.int32),
            pltpu.SMEM(tile, jnp.int32),
            pltpu.SMEM(tile, jnp.int32),
            pltpu.SMEM((columns,) + tile, jnp.int32),
            pltpu.SMEM(tile, jnp.int32),
        ]
        + [dma(())]
        + [zs] * 4
        + [dma((2, 2))] * 2
        + [ys] * 4
        + [dma(())] * 2
        + [dma((2, columns))] * 2
        + [dma((2,))] * 2
        + [dma((4,))] * 2
        + [dma((3,))],
        compiler_params=pltpu.CompilerParams(collective_id=0, has_side_effects=True),
    )(meta, prior, a1_blocks, pieces)


def solution(mesh):
    placed = (
        P("rows", "cols", None, None),
        P("rows", "cols"),
        P(("rows", "cols")),
        P(("rows", "cols"), None, None, None),
        P(("rows", "cols"), None, None),
    )
    return jax.shard_map(
        local, mesh=mesh, in_specs=placed, out_specs=P("rows", "cols", None, None), check_vma=False
    )
```

```python
import jax
import jax.numpy as jnp
from jax import lax
from jax.experimental import pallas as pl
from jax.experimental.pallas import tpu as pltpu
from jax.sharding import PartitionSpec as P

mixing = 0.75


def contract(a, b, dims):
    return lax.dot_general(a, b, (dims, ((), ())), preferred_element_type=jnp.float32)


MESH = pl.DeviceIdType.MESH
ny, nz, cores = 4, 16, 2
hops = (9, 6)


def propagate_kernel(
    meta, prior, a1, a2, out,
    whole, adjacency, next_prior, first, next_first, next_meta, col_meta,
    my_ids, next_ids, links, picks,
    own_sem, az_s, az_r, bz_s, bz_r, by_s, by_r, ay_s, ay_r, ah_s, ah_r, sib_s, sib_r,
    col_s, col_r, next_s, next_r, first_s, first_r, local_sem,
):
    rows, per, block = prior.shape[0], prior.shape[1], prior.shape[2]
    upper = rows // 2
    columns = adjacency.shape[0]
    row_share = rows // columns
    me, col = lax.axis_index("rows"), lax.axis_index("cols")
    core = lax.rem(me, cores)
    z = lax.rem(me // cores, nz)
    y = me // (cores * nz)
    height = a2.shape[0]
    cut = height * 3 // 4
    a_half, b_half = cut // 2, (height - cut) // 2
    a_all, b_all = pl.ds(0, cut), pl.ds(cut, height - cut)
    a_part = (pl.ds(0, a_half), pl.ds(a_half, a_half))
    b_part = (pl.ds(cut, b_half), pl.ds(cut + b_half, b_half))

    def zz(by):
        return lax.rem(z + by + nz, nz)

    def yy(by):
        return lax.rem(y + by + ny, ny)

    def device(y_at, z_at, core_at):
        return ((y_at * nz + z_at) * cores + core_at, col)

    z_to = (device(y, zz(1), core), device(y, zz(-1), core))
    y_to = (device(yy(1), z, core), device(yy(-1), z, core))
    sibling = device(y, z, 1 - core)
    sign = (-1, 1)
    slabs = ny * nz * cores
    before = (lax.rem(me + slabs - 1, slabs), col)
    after = (lax.rem(me + 1, slabs), col)
    col_to = tuple((me, lax.rem(col + by, columns)) for by in range(1, columns))

    barrier = pltpu.get_barrier_semaphore()
    for other in z_to + y_to + (sibling, before, after) + col_to:
        pl.semaphore_signal(barrier, inc=1, device_id=other, device_id_type=MESH)
    own = pltpu.make_async_copy(a2, whole.at[y, z, core], own_sem)
    own.start()
    own_a1 = pltpu.make_async_copy(a1, adjacency.at[col], local_sem.at[0])
    own_a1.start()
    own_links = pltpu.make_async_copy(meta, links.at[col], local_sem.at[1])
    own_links.start()
    own_ids = pltpu.make_async_copy(meta, my_ids, local_sem.at[2])
    own_ids.start()
    pl.semaphore_wait(barrier, 7 + columns - 1)

    def copy(src, dst, send_sem, recv_sem, to):
        return pltpu.make_async_remote_copy(
            src_ref=src, dst_ref=dst, send_sem=send_sem, recv_sem=recv_sem,
            device_id=to, device_id_type=MESH,
        )

    def az(d, s, part, mine=False):
        place = whole.at[y, zz(sign[d] * (s - 1)), core, part]
        return copy(a2.at[part] if mine else place, place, az_s.at[d, s], az_r.at[d, s], z_to[d])

    def az_in(d, s, part):
        place = whole.at[y, zz(sign[d] * s), core, part]
        copy(place, place, az_s.at[d, s], az_r.at[d, s], z_to[d]).wait_recv()

    def bz(d, s, part):
        place = whole.at[:, zz(sign[d] * (s - 1)), core, part]
        return copy(place, place, bz_s.at[d, s], bz_r.at[d, s], z_to[d])

    def bz_in(d, s, part):
        place = whole.at[:, zz(sign[d] * s), core, part]
        copy(place, place, bz_s.at[d, s], bz_r.at[d, s], z_to[d]).wait_recv()

    def by(d, h, y_at, part, mine=False):
        place = whole.at[y_at, z, core, part]
        return copy(a2.at[part] if mine else place, place, by_s.at[d, h], by_r.at[d, h], y_to[d])

    def ay(d, z_at, mine=False):
        place = whole.at[y, z_at, core, a_all]
        return copy(a2.at[a_all] if mine else place, place, ay_s.at[d, z_at], ay_r.at[d, z_at], y_to[d])

    def ay_in(d, z_at):
        place = whole.at[yy(sign[d]), z_at, core, a_all]
        copy(place, place, ay_s.at[d, z_at], ay_r.at[d, z_at], y_to[d]).wait_recv()

    def ah(d, y_at, z_at):
        place = whole.at[y_at, z_at, core, a_part[d]]
        return copy(place, place, ah_s.at[d, z_at], ah_r.at[d, z_at], y_to[d])

    def share(place):
        copy(place, place, sib_s, sib_r, sibling).start()

    def from_y(z_at):
        for d in range(2):
            ay_in(d, z_at)
            ah(d, yy(sign[d]), z_at).start()
            share(whole.at[yy(sign[d]), z_at, core, a_all])

    def from_y_far(z_at):
        for d in range(2):
            ah(d, yy(2), z_at).wait_recv()
        share(whole.at[yy(2), z_at, core, a_all])

    def going(s):
        return [d for d in range(2) if s <= hops[d]]

    def sources(s):
        return [zz(sign[d] * s) for d in going(s)] if s else [z]

    def a_step(s):
        for d in going(s):
            z_at = zz(sign[d] * s)
            az_in(d, s, a_all)
            if s < hops[d]:
                az(d, s + 1, a_all).start()
            for e in range(2):
                ay(e, z_at).start()
            share(whole.at[y, z_at, core, a_all])

    def b_step(s):
        for d in going(s):
            z_at = zz(sign[d] * s)
            bz_in(d, s, b_all)
            if s < hops[d]:
                bz(d, s + 1, b_all).start()
            share(whole.at[:, z_at, core, b_all])

    def col_a1(by, source):
        return copy(a1, adjacency.at[source], col_s.at[0, by], col_r.at[0, by], col_to[by - 1])

    def col_links(by, source):
        return copy(meta, col_meta.at[source], col_s.at[1, by], col_r.at[1, by], col_to[by - 1])

    def ids_along():
        return copy(meta, next_meta, next_s.at[0], next_r.at[0], before)

    pair = upper // 4

    def prior_along(part):
        here = prior.at[pl.ds(upper + part * pair, pair)]
        there = next_prior.at[pl.ds(part * pair, pair)]
        return copy(here, there, next_s.at[1 + part], next_r.at[1 + part], before)

    def first_along(part):
        here = first.at[pl.ds(upper + part * pair, pair)]
        there = next_first.at[pl.ds(part * pair, pair)]
        return copy(here, there, first_s.at[part], first_r.at[part], before)

    def left_row(i):
        owner, at = i // row_share, lax.rem(i, row_share)
        linked = lax.rem(links[owner, 1, at], upper)
        for k in range(per):
            n = i * per + k
            target = my_ids[0, n]
            chosen, found = jnp.int32(0), jnp.int32(0)
            for j in range(per):
                same = (next_ids[0, (linked + upper) * per + j] == target).astype(jnp.int32)
                chosen = chosen + same * j
                found = found + same
            picks[0, n] = linked
            chosen = lax.rem(chosen, per)
            picks[1, n] = chosen
            picks[2, n] = found
            picked = next_prior[linked, chosen]
            total = contract(adjacency[owner, at, 0], prior[i, k], ((1,), (0,)))
            cross = contract(adjacency[owner, at, 1], picked, ((1,), (0,)))
            total = total + cross * found.astype(jnp.float32)
            first[i, k] = total.astype(jnp.bfloat16)

    def target_of(n):
        name = my_ids[0, n]
        slab = lax.div(name, columns * targets)
        slab_y, slab_z = lax.div(slab, nz * cores), lax.rem(lax.div(slab, cores), nz)
        slab_core, low = lax.rem(slab, cores), lax.rem(name, targets) * 2
        upper_part = whole[slab_y, slab_z, slab_core, low]
        return jnp.concatenate([upper_part, whole[slab_y, slab_z, slab_core, low + 1]], axis=0)

    def square(a, b, c, d):
        top, bottom = jnp.concatenate([a, b], axis=1), jnp.concatenate([c, d], axis=1)
        return jnp.concatenate([top, bottom], axis=0)

    def sweep_row(i, carry):
        owner, at = i // row_share, lax.rem(i, row_share)
        weights = jnp.concatenate([adjacency[owner, at, 0], adjacency[owner, at, 1]], axis=1)
        for k in range(0, per, 2):
            n, m = i * per + k, i * per + k + 1
            one, two = target_of(n), target_of(m)
            zero = jnp.zeros_like(one)
            both = square(one, zero, zero, two)
            values = square(
                first[i, k],
                first[i, k + 1],
                next_first[picks[0, n], picks[1, n]],
                next_first[picks[0, m], picks[1, m]],
            )
            base = square(
                prior[i, k],
                prior[i, k + 1],
                next_prior[picks[0, n], picks[1, n]],
                next_prior[picks[0, m], picks[1, m]],
            ).astype(jnp.float32)
            image = contract(values, both, ((1,), (1,)))
            swept = (mixing * image + (1.0 - mixing) * base).astype(jnp.bfloat16)
            carried = contract(swept, both, ((1,), (1,)))
            stacked = square(
                carried[:block, :block],
                carried[:block, block:],
                carried[block:, :block] * picks[2, n].astype(jnp.float32),
                carried[block:, block:] * picks[2, m].astype(jnp.float32),
            ).astype(jnp.bfloat16)
            total = contract(weights, stacked, ((1,), (0,)))
            mixed = (mixing * total + (1.0 - mixing) * base[:block]).astype(jnp.bfloat16)
            out[i, k] = mixed[:, :block]
            out[i, k + 1] = mixed[:, block:]
        return carry

    def left_rows(s):
        def one(i, carry):
            left_row(upper + s * pair + i)
            left_row(s * pair + i)
            return carry

        lax.fori_loop(0, pair, one, 0)

    targets = whole.shape[3] // 2
    ids_along().start()
    for by_col in range(1, columns):
        col_links(by_col, col).start()
        col_a1(by_col, col).start()
    for d in range(2):
        az(d, 1, a_all, True).start()
        by(d, 0, y, b_all, True).start()
    for d in range(2):
        ay(d, z, True).start()
    for d in range(2):
        by(d, 0, yy(sign[d]), b_all).wait_recv()
        by(d, 1, yy(sign[d]), b_part[d]).start()
    own.wait()
    share(whole.at[y, z, core, a_all])
    a_step(1)
    for d in range(2):
        by(d, 1, yy(2), b_part[d]).wait_recv()
    for d in range(2):
        bz(d, 1, b_all).start()
    share(whole.at[:, z, core, b_all])
    def ready():
        own_ids.wait()
        own_links.wait()
        own_a1.wait()
        ids_along().wait_recv()
        to_smem = pltpu.make_async_copy(next_meta, next_ids, local_sem.at[2])
        to_smem.start()
        for by_col in range(1, columns):
            source = lax.rem(col + columns - by_col, columns)
            col_links(by_col, source).wait_recv()
            moved = pltpu.make_async_copy(col_meta.at[source], links.at[source], local_sem.at[1])
            moved.start()
            moved.wait()
            col_a1(by_col, source).wait_recv()
        to_smem.wait()
        for part in range(4):
            prior_along(part).wait_recv()

    longest = max(hops)
    for s in range(2, longest + 5):
        a_step(s)
        b_step(s - 1)
        if 3 <= s < 7:
            prior_along(s - 3).start()
        if 9 <= s < 13:
            first_along(s - 9).start()
        for z_at in sources(s - 2):
            from_y(z_at)
        if s >= 4:
            for z_at in sources(s - 4):
                from_y_far(z_at)
        if s == 8:
            ready()
        if 8 <= s < 12:
            left_rows(s - 8)
    for d in range(2):
        by(d, 0, y, b_all).wait_send()
        by(d, 1, y, b_part[d]).wait_send()

        def sent_z(s, carry, d=d):
            az(d, s, a_all).wait_send()
            bz(d, s, b_all).wait_send()
            return carry

        lax.fori_loop(1, hops[d] + 1, sent_z, 0)

    def sent_y(z_at, carry):
        for d in range(2):
            ay(d, z_at).wait_send()
            ah(d, y, z_at).wait_send()
        return carry

    lax.fori_loop(0, nz, sent_y, 0)
    mine, theirs = whole.at[:, :, core], whole.at[:, :, 1 - core]
    copy(mine, mine, sib_s, sib_r, sibling).wait_send()
    copy(theirs, theirs, sib_s, sib_r, sibling).wait_recv()
    ids_along().wait_send()
    for part in range(4):
        prior_along(part).wait_send()
    for by_col in range(1, columns):
        col_links(by_col, col).wait_send()
        col_a1(by_col, col).wait_send()
    for part in range(4):
        first_along(part).wait_send()
        first_along(part).wait_recv()
    lax.fori_loop(0, rows, sweep_row, 0)


def local(prior, candidates, cross_link, a1_blocks, a2_blocks):
    rows, per, block = prior.shape[0], prior.shape[1], prior.shape[2]
    columns = lax.axis_size("cols")
    targets_here = a2_blocks.shape[0]
    upper = rows // 2
    pieces = a2_blocks.reshape(2 * targets_here, block // 2, block)
    lanes = 128
    ids = jnp.pad(candidates.reshape(1, -1), ((0, 0), (0, lanes - candidates.size)))
    names = jnp.pad(cross_link.reshape(1, -1), ((0, 6), (0, lanes - cross_link.size)))
    meta = jnp.concatenate([ids, names], axis=0)
    tile = meta.shape
    dma = pltpu.SemaphoreType.DMA
    zs, ys = dma((2, max(hops) + 1)), dma((2, nz))
    vmem = pl.BlockSpec(memory_space=pltpu.VMEM)
    half = (upper,) + prior.shape[1:]
    return pl.pallas_call(
        propagate_kernel,
        out_shape=jax.ShapeDtypeStruct(prior.shape, prior.dtype),
        in_specs=[vmem] * 4,
        out_specs=vmem,
        scratch_shapes=[
            pltpu.VMEM((ny, nz, cores) + pieces.shape, jnp.bfloat16),
            pltpu.VMEM((columns,) + a1_blocks.shape, jnp.bfloat16),
            pltpu.VMEM(half, jnp.bfloat16),
            pltpu.VMEM(prior.shape, jnp.bfloat16),
            pltpu.VMEM(half, jnp.bfloat16),
            pltpu.VMEM(tile, jnp.int32),
            pltpu.VMEM((columns,) + tile, jnp.int32),
            pltpu.SMEM(tile, jnp.int32),
            pltpu.SMEM(tile, jnp.int32),
            pltpu.SMEM((columns,) + tile, jnp.int32),
            pltpu.SMEM(tile, jnp.int32),
        ]
        + [dma(())]
        + [zs] * 4
        + [dma((2, 2))] * 2
        + [ys] * 4
        + [dma(())] * 2
        + [dma((2, columns))] * 2
        + [dma((5,))] * 2
        + [dma((4,))] * 2
        + [dma((3,))],
        compiler_params=pltpu.CompilerParams(collective_id=0, has_side_effects=True),
    )(meta, prior, a1_blocks, pieces)


def solution(mesh):
    placed = (
        P("rows", "cols", None, None),
        P("rows", "cols"),
        P(("rows", "cols")),
        P(("rows", "cols"), None, None, None),
        P(("rows", "cols"), None, None),
    )
    return jax.shard_map(
        local, mesh=mesh, in_specs=placed, out_specs=P("rows", "cols", None, None), check_vma=False
    )
```
